32 devices in a mesh: segment: 1, expert: 32 (over z, y, x, core).
Axes of the slice: x: 2, y: 2, z: 4, core: 2. Of those that a mesh axis runs over, the one named last changes fastest.
Arguments:
- tokens: bfloat16 [1, 768, 3584], P('segment', 'expert'), may hold values from -36 to 36
- routes: int32 [1, 768, 2], P('segment', 'expert'), may hold values from 0 to 3, all different within a row; in each aligned block of 24 rows (0 to 23, 24 to 47, ..., all dimensions but the last counted through in order) at most 24 rows name the same one
- norm_gain: bfloat16 [1, 3584], P('segment'), may hold values from 0.099609375 to 1.8984375
- router: bfloat16 [1, 3584, 4], P('segment'), may hold values from -0.09375 to 0.09375
- gate_values: bfloat16 [1, 3584, 4096], P('segment', None, 'expert'), may hold values from -0.09375 to 0.09375
- gate_scale: float32 [1, 28, 32], P('segment', None, 'expert'), may hold values from 0.5 to 2
- up_values: bfloat16 [1, 3584, 4096], P('segment', None, 'expert'), may hold values from -0.09375 to 0.09375
- up_scale: float32 [1, 28, 32], P('segment', None, 'expert'), may hold values from 0.5 to 2
- down_values: bfloat16 [1, 4096, 3584], P('segment', 'expert'), may hold values from -0.1875 to 0.1875
- down_scale: float32 [1, 32, 28], P('segment', 'expert'), may hold values from 0.5 to 2
Outputs:
- arriving: bfloat16 [1, 768, 3584], P('segment', 'expert')
The draws below stay inside these ranges and needn't reach their ends.
Inputs may be any that keep to these rules, and one draw needn't show every extreme that they name: `routes`: in the rows of one device each expert is named at most 24 times, and a row names 2 different experts.
All inputs are finite; a program needn't handle non-finite values.
Results may differ from the reference program's by a relative error of at most 0.0081.
Values may be sent and summed in bfloat16 or wider, within the bound.
A program may use at most 64 MiB of HBM per device.

```python
import math
import jax
import jax.numpy as jnp
import numpy as np
from jax import lax

D = 3584
FF = 1024
GROUP = 8
BLOCK = 128
TOPK = 2
TOK_DEV = 24
SEGMENTS = 1
TOKENS = 768
EXPERTS = 4
FF_DEV = 128
CAP = 24


def draw_tokens(key, part):
    first_key, row_key, col_key = jax.random.split(key, 3)
    rows = jnp.exp(jax.random.uniform(row_key, (SEGMENTS, TOKENS, 1), jnp.float32, math.log(0.3), math.log(3.0)))
    cols = jnp.exp(jax.random.uniform(col_key, (1, 1, D), jnp.float32, math.log(0.3), math.log(3.0)))
    base = jnp.clip(jax.random.normal(first_key, (SEGMENTS, TOKENS, D), jnp.float32), -4.0, 4.0)
    return (base * rows * cols).astype(jnp.bfloat16)


def block_levels(own_key, shape, cuts, low, high):
    level, own = 1.0, jax.random.fold_in(own_key, 6)
    for dim, parts in cuts:
        steps = jnp.exp(jax.random.uniform(jax.random.fold_in(own, dim), (parts,), jnp.float32, low / len(cuts), high / len(cuts)))
        level = level * jnp.repeat(steps, shape[dim] // parts).reshape([-1 if axis == dim else 1 for axis in range(len(shape))])
    return level


def shared_out(rng, own, number, rows, number_of, top, bound, slope):
    order = jax.random.permutation(rng, number_of)
    packed, ordinary = shares(number_of, rows * top, bound, slope, True), shares(number_of, rows * top, bound, slope, False)
    places = jnp.arange(number_of)

    def named(lengths, offset_by):
        used = int((lengths > 0).sum())
        fixed = max(1, used // 4)
        moved = fixed + (places - fixed + offset_by * (used - fixed)) % max(1, number_of - fixed)
        return jnp.zeros((number_of,), jnp.int32).at[order[jnp.where(places < fixed, places, moved)]].set(jnp.asarray(lengths, jnp.int32))

    lengths = jnp.where(number % 4 == 0, named(packed, number // 4), named(ordinary, number - number // 4 - 1))
    mixed = jax.random.permutation(jax.random.fold_in(own, 3), number_of)
    source_of, sink = mixed[0:number_of // 2 * 2:2], mixed[1:number_of // 2 * 2:2]
    margin = jnp.minimum(lengths[source_of] - 1, bound - lengths[sink]) // 2
    margin = jnp.where((source_of == order[0]) | (sink == order[0]) | (lengths[sink] == 0), 0, jnp.maximum(margin, 0))
    moved = jax.random.randint(jax.random.fold_in(own, 4), (number_of // 2,), 0, 1 << 20) % (margin + 1)
    lengths = lengths.at[source_of].add(-moved).at[sink].add(moved)
    members = jnp.searchsorted(jnp.cumsum(lengths), jnp.arange(rows * top), side="right").astype(jnp.int32)
    grid = members.reshape(top, rows).T
    grid = grid[jax.random.permutation(jax.random.fold_in(own, 1), rows)]
    offset_by = jax.random.randint(jax.random.fold_in(own, 2), (rows, 1), 0, top)
    return jnp.take_along_axis(grid, (jnp.arange(top)[None, :] + offset_by) % top, axis=1)


def shares(amount, total, limit, lean, full):
    loads = [(1 << 20) // math.isqrt(rank ** lean) + 1 for rank in range(1, amount + 1)]
    largest = limit if full else min(limit, max(-(-total // amount), total * loads[0] // sum(loads)))
    least = 1 if total - largest >= amount - 1 else 0
    holding, spare = [largest] + [least] * (amount - 1), total - largest - least * (amount - 1)
    while spare > 0:
        free = [i for i in range(1, amount) if holding[i] < largest] or [i for i in range(1, amount) if holding[i] < limit]
        whole, remaining = sum([loads[i] for i in free]), spare
        for i in free:
            more = min(limit - holding[i], max(1, remaining * loads[i] // whole), spare)
            holding[i] = holding[i] + more
            spare = spare - more
    return np.array(holding)


def centred(own_key, dims, spread, limit, cuts=(), kind=jnp.bfloat16):
    entries = jax.random.normal(own_key, dims, jnp.float32) * spread
    if len(cuts) > 0:
        entries = block_levels(own_key, dims, cuts, -0.22, 0.18) * entries
    return jnp.clip(entries, min=-limit, max=limit).astype(kind)


def setup_inputs(seed: int = 0) -> dict:
    streams_of = jax.random.split(jax.random.key(seed), 11)
    tokens = draw_tokens(jax.random.fold_in(streams_of[10], 71), 0)
    routes_keys = jax.random.split(jax.random.fold_in(streams_of[1], 1), SEGMENTS * TOKENS // TOK_DEV)
    routes_turns = jax.random.permutation(jax.random.fold_in(streams_of[1], 3), SEGMENTS * TOKENS // TOK_DEV)
    routes = jax.vmap(lambda own, number: shared_out(jax.random.fold_in(streams_of[1], 2), own, number, TOK_DEV, EXPERTS, TOPK, CAP, 2))(routes_keys, routes_turns).reshape((SEGMENTS, TOKENS, TOPK))
    norm_gain = jnp.clip(1.0 + 0.18 * jax.random.normal(streams_of[2], (SEGMENTS, D), jnp.float32), 0.099609375, 1.8984375).astype(jnp.bfloat16)
    router = centred(streams_of[3], (SEGMENTS, D, EXPERTS), D ** -0.5, 0.09375)
    gate_values = centred(streams_of[4], (SEGMENTS, D, EXPERTS * FF), D ** -0.5, 0.09375, ((2, 32),))
    gate_scale = jnp.clip(jnp.exp(math.log(2.0) - 1.3862944 * jax.random.uniform(streams_of[5], (SEGMENTS, D // BLOCK, EXPERTS * FF // BLOCK), jnp.float32) ** block_levels(streams_of[5], (SEGMENTS, D // BLOCK, EXPERTS * FF // BLOCK), ((2, 32),), -0.2, 0.2)), 0.5, 2.0)
    up_values = centred(streams_of[6], (SEGMENTS, D, EXPERTS * FF), D ** -0.5, 0.09375, ((2, 32),))
    up_scale = jnp.clip(jnp.exp(math.log(2.0) - 1.3862944 * jax.random.uniform(streams_of[7], (SEGMENTS, D // BLOCK, EXPERTS * FF // BLOCK), jnp.float32) ** block_levels(streams_of[7], (SEGMENTS, D // BLOCK, EXPERTS * FF // BLOCK), ((2, 32),), -0.2, 0.2)), 0.5, 2.0)
    down_values = centred(streams_of[8], (SEGMENTS, EXPERTS * FF, D), FF ** -0.5, 0.1875, ((1, 32),))
    down_scale = jnp.clip(jnp.exp(math.log(2.0) - 1.3862944 * jax.random.uniform(streams_of[9], (SEGMENTS, EXPERTS * FF // BLOCK, D // BLOCK), jnp.float32) ** block_levels(streams_of[9], (SEGMENTS, EXPERTS * FF // BLOCK, D // BLOCK), ((1, 32),), -0.2, 0.2)), 0.5, 2.0)
    return {"tokens": tokens, "routes": routes, "norm_gain": norm_gain, "router": router, "gate_values": gate_values, "gate_scale": gate_scale, "up_values": up_values, "up_scale": up_scale, "down_values": down_values, "down_scale": down_scale}


ROUTE_SCALE = 2.5
EPSILON = 1e-06

def dequantize(values, scales):
    wide = jnp.repeat(jnp.repeat(scales, BLOCK, axis=0), BLOCK, axis=1)
    return (values.astype(jnp.float32) * wide).astype(jnp.bfloat16)

def segment_layer(operands):
    hidden_in, picks, gain, route_cols, gate_vals, gate_scl, upper_vals, upper_scl, down_vals, down_scl = operands
    residual = hidden_in.astype(jnp.float32)
    normed = (residual * lax.rsqrt(lax.optimization_barrier(jnp.mean(residual * residual, -1, keepdims=True)) + EPSILON) * gain.astype(jnp.float32)).astype(jnp.bfloat16)
    affinity = jax.nn.sigmoid(jnp.dot(normed, route_cols, preferred_element_type=jnp.float32))
    chosen_mask = picks[:, :, None] == jnp.arange(EXPERTS, dtype=jnp.int32)[None, None, :]
    chosen = lax.optimization_barrier(jnp.sum(jnp.where(chosen_mask, affinity[:, None, :], 0.0), -1))
    share = ROUTE_SCALE * chosen / lax.optimization_barrier(jnp.sum(chosen, -1, keepdims=True))
    coef_all = lax.optimization_barrier(jnp.sum(jnp.where(chosen_mask, share[:, :, None], 0.0), 1))

    def one_expert(total, index):
        first = index * FF
        block_first = index * (FF // BLOCK)
        w_gate = dequantize(lax.dynamic_slice_in_dim(gate_vals, first, FF, 1), lax.dynamic_slice_in_dim(gate_scl, block_first, FF // BLOCK, 1))
        w_upper = dequantize(lax.dynamic_slice_in_dim(upper_vals, first, FF, 1), lax.dynamic_slice_in_dim(upper_scl, block_first, FF // BLOCK, 1))
        w_down = dequantize(lax.dynamic_slice_in_dim(down_vals, first, FF, 0), lax.dynamic_slice_in_dim(down_scl, block_first, FF // BLOCK, 0))
        gate = jnp.dot(normed, w_gate, preferred_element_type=jnp.float32)
        upward = jnp.dot(normed, w_upper, preferred_element_type=jnp.float32)
        hidden = (jax.nn.silu(gate) * upward).astype(jnp.bfloat16)
        pieces = jnp.einsum('tgf,gfd->tgd', hidden.reshape(-1, GROUP, FF_DEV).astype(jnp.float32), w_down.reshape(GROUP, FF_DEV, D).astype(jnp.float32))
        rounded = lax.optimization_barrier(pieces.astype(jnp.bfloat16))
        expert_out = lax.optimization_barrier(jnp.sum(rounded.astype(jnp.float32), 1))
        coef = lax.dynamic_slice_in_dim(coef_all, index, 1, 1)
        return (total + coef * expert_out, None)
    start = jnp.zeros((hidden_in.shape[0], D), jnp.float32)
    total, unused = lax.scan(one_expert, start, jnp.arange(EXPERTS, dtype=jnp.int32))
    return (residual + total).astype(jnp.bfloat16)

def reference(tokens, routes, norm_gain, router, gate_values, gate_scale, up_values, up_scale, down_values, down_scale):
    results = lax.map(segment_layer, (tokens, routes, norm_gain, router, gate_values, gate_scale, up_values, up_scale, down_values, down_scale))
    return jnp.roll(results, 1, axis=0)
```

```python
import functools

import jax
import jax.numpy as jnp
from jax import lax
from jax.experimental import pallas as pl
from jax.experimental.pallas import tpu as pltpu
from jax.sharding import PartitionSpec as P

BLOCK = 128
ROUTE_SCALE = 2.5
EPSILON = 1e-06

ORDER = (0, 2, 4, 6, 1, 3, 5, 7)
CORE, NEAR_X, NEAR_Y = 1, 2, 4
RELIEF = 0.36

SLOTS = {
    "core_own": {0: 0, 1: 27, 2: 30, 3: 53},
    "y_low": {0: 1, 1: 31, 2: 16, 3: 39},
    "xp": {0: 2},
    "spread": {1: 3, 2: 6, 3: 17},
    "yp": {0: 4},
    "x_low": {0: 5, 1: 24, 2: 20, 3: 43},
    "y_high": {0: 7, 1: 25, 2: 18, 3: 48},
    "fp_lo": {0: 8},
    "x_high": {0: 9, 1: 23, 2: 19, 3: 47},
    "far_low": {0: 10, 1: 34, 2: 28, 3: 57},
    "rel4": {1: 37, 2: 11, 3: 42},
    "core_x": {0: 12, 1: 52, 2: 41, 3: 66},
    "rel2": {1: 33, 2: 13, 3: 46},
    "far_high": {0: 14, 1: 35, 2: 26, 3: 56},
    "fp_hi": {0: 15},
    "core_far": {0: 21, 1: 58, 2: 49, 3: 65},
    "core_y": {0: 22, 1: 55, 2: 45, 3: 60},
    "rel6": {1: 40, 2: 29, 3: 51},
    "comp": {0: 32, 1: 64, 2: 54, 3: 70},
    "diag_high": {0: 36, 1: 71, 2: 61, 3: 73},
    "sum_x_low": {0: 38, 1: 77, 2: 63, 3: 82},
    "diag_low": {0: 44, 1: 69, 2: 59, 3: 72},
    "sum_y_high": {0: 50, 1: 81, 2: 62, 3: 74},
    "sum_y_low": {0: 85, 1: 78, 2: 67, 3: 84},
    "sum_x_high": {0: 83, 1: 80, 2: 68, 3: 79},
    "homeh": {1: 90, 2: 75, 3: 86},
    "homel": {1: 87, 2: 76, 3: 89},
    "finh": {0: 93, 1: 97, 2: 88, 3: 92},
    "finl": {0: 94, 1: 95, 2: 91, 3: 96},
}


def flipped(index, bits):
    out = index
    bit = 1
    while bit <= bits:
        if bits & bit:
            out = out + bit - 2 * bit * ((index // bit) % 2)
        bit *= 2
    return out


def steps(experts):
    needs = {}
    for s in range(experts):
        parent = s - (s & -s)
        if s:
            needs["spread", s] = [("spread", parent)] if parent else []
            for q, got in (("2", ["xp"]), ("4", ["yp"]), ("6", ["fp_lo", "fp_hi"])):
                needs["rel" + q, s] = [("rel" + q, parent)] if parent else [(k, 0) for k in got]
        else:
            needs.update({("xp", 0): [], ("yp", 0): [], ("fp_lo", 0): [("xp", 0)], ("fp_hi", 0): [("yp", 0)]})
        arrived = [("spread", s)] if s else []
        got = {
            q: [("rel" + q, s)] if s else [(k, 0) for k in first]
            for q, first in (("2", ["xp"]), ("4", ["yp"]), ("6", ["fp_lo", "fp_hi"]))
        }
        for kind in ("x_low", "y_high", "x_high", "y_low", "core_own"):
            needs[kind, s] = list(arrived)
        needs["far_low", s] = [("x_low", s)]
        needs["far_high", s] = [("y_high", s)]
        needs["core_x", s] = [("x_low", s), ("x_high", s)] + got["2"]
        needs["core_y", s] = [("y_low", s), ("y_high", s)] + got["4"]
        needs["core_far", s] = [("far_low", s), ("far_high", s)] + got["6"]
        needs["comp", s] = (
            arrived
            + needs["core_x", s]
            + needs["core_y", s]
            + needs["core_far", s]
            + [(k, s) for k in ("core_own", "core_x", "core_y", "core_far")]
        )
        low, high = [("comp", s), ("swap_low", s)], [("comp", s), ("swap_high", s)]
        needs["diag_low", s] = needs["sum_x_low", s] = low
        needs["diag_high", s] = needs["sum_y_high", s] = high
        needs["sum_y_low", s] = low + [("diag_low", s)]
        needs["sum_x_high", s] = high + [("diag_high", s)]
        for part, half in (("l", "low"), ("h", "high")):
            sums = [("comp", s), ("swap_" + half, s), ("sum_x_" + half, s), ("sum_y_" + half, s)]
            if s:
                needs["home" + part, s] = sums
                needs["fin" + part, s] = [("home" + part, s)]
            else:
                needs["fin" + part, s] = sums
    return needs


def plan(experts):
    needs = steps(experts)
    if all(kind in SLOTS and s in SLOTS[kind] for kind, s in needs) and experts == len(SLOTS["comp"]):
        return needs, sorted(needs, key=lambda step: SLOTS[step[0]][step[1]])
    depth = {}

    def level(step):
        if step not in depth:
            made = ("comp", step[1]) if step[0].startswith("swap") else None
            before = [made] if made else needs[step]
            depth[step] = 1 + max((level(b) for b in before), default=0)
        return depth[step]

    return needs, sorted(needs, key=lambda step: (level(step), step[1]))


def kinds(experts):
    needs, _ = plan(experts)
    local = ("comp", "finl", "finh")
    return [step for step in needs if step[0] not in local] + [
        (kind, s) for kind in ("swap_low", "swap_high") for s in range(experts)
    ]


def kernel(
    experts,
    group,
    gate_scale,
    up_scale,
    down_scale,
    tokens,
    picks,
    gain,
    router,
    gate_values,
    up_values,
    down_values,
    out,
    rows,
    part,
    core_in,
    diag_x,
    diag_y,
    full_x,
    full_y,
    homed,
    w_in,
    w_down,
    gate_raw,
    up_raw,
    down_raw,
    acc,
    send_sem,
    recv_sem,
    load_sem,
):
    tok_dev, width = tokens.shape[1:]
    blocks = width // BLOCK
    half = blocks // 2 * BLOCK
    low, high = pl.ds(0, half), pl.ds(half, width - half)
    relief = int(blocks * RELIEF) // 2 * 2
    split = relief + (blocks - relief) // 2
    p_all, p_lo, p_hi = (
        pl.ds(a * BLOCK, (b - a) * BLOCK)
        for a, b in ((0, relief), (0, relief // 2), (relief // 2, relief))
    )
    z_lo, z_hi = pl.ds(relief * BLOCK, (split - relief) * BLOCK), pl.ds(split * BLOCK, (blocks - split) * BLOCK)
    me = lax.axis_index("expert")
    core, near_x, near_y = flipped(me, CORE), flipped(me, NEAR_X), flipped(me, NEAR_Y)
    planes = [flipped(me, s * group) for s in range(experts)]

    loads = [
        pltpu.make_async_copy(src.at[0], dst, load_sem.at[i])
        for i, (src, dst) in enumerate(
            ((gate_values, gate_raw), (up_values, up_raw), (down_values, down_raw))
        )
    ]

    barrier = pltpu.get_barrier_semaphore()
    partners = [core, near_x, near_y] + planes[1:]
    for other in partners:
        pl.semaphore_signal(
            barrier, inc=1, device_id={"expert": other}, device_id_type=pl.DeviceIdType.MESH
        )
    for load in loads:
        load.start()

    def at(q):
        return pl.ds(ORDER.index(q) * tok_dev, tok_dev)

    odd = pl.ds(group // 2 * tok_dev, group // 2 * tok_dev)
    numbers = {step: i for i, step in enumerate(kinds(experts))}

    def ends(kind, s):
        g, p = rows.at[s], part.at[s]
        toward = s & -s
        if kind == "spread":
            return rows.at[s - toward, at(0)], g.at[at(0)], planes[toward]
        if kind.startswith("rel"):
            q = int(kind[3:])
            return rows.at[s - toward, at(q), p_all], g.at[at(q), p_all], planes[toward]
        if kind.startswith("home"):
            columns = low if kind == "homel" else high
            return p.at[at(0), columns], homed.at[s, :, columns], planes[s]
        return {
            "xp": lambda: (g.at[at(0), p_all], g.at[at(2), p_all], near_x),
            "yp": lambda: (g.at[at(0), p_all], g.at[at(4), p_all], near_y),
            "fp_lo": lambda: (g.at[at(2), p_lo], g.at[at(6), p_lo], near_y),
            "fp_hi": lambda: (g.at[at(4), p_hi], g.at[at(6), p_hi], near_x),
            "x_low": lambda: (g.at[at(0), z_lo], g.at[at(2), z_lo], near_x),
            "x_high": lambda: (g.at[at(0), z_hi], g.at[at(2), z_hi], near_x),
            "y_low": lambda: (g.at[at(0), z_lo], g.at[at(4), z_lo], near_y),
            "y_high": lambda: (g.at[at(0), z_hi], g.at[at(4), z_hi], near_y),
            "far_low": lambda: (g.at[at(2), z_lo], g.at[at(6), z_lo], near_y),
            "far_high": lambda: (g.at[at(4), z_hi], g.at[at(6), z_hi], near_x),
            "core_own": lambda: (g.at[at(0)], g.at[at(1)], core),
            "core_x": lambda: (g.at[at(2)], g.at[at(3)], core),
            "core_y": lambda: (g.at[at(4)], g.at[at(5)], core),
            "core_far": lambda: (g.at[at(6)], g.at[at(7)], core),
            "swap_low": lambda: (p.at[odd, low], core_in.at[s, :, low], core),
            "swap_high": lambda: (p.at[odd, high], core_in.at[s, :, high], core),
            "diag_low": lambda: (p.at[at(6), low], diag_x.at[s], near_x),
            "diag_high": lambda: (p.at[at(6), high], diag_y.at[s], near_y),
            "sum_x_low": lambda: (p.at[at(2), low], full_x.at[s, :, low], near_x),
            "sum_x_high": lambda: (p.at[at(2), high], full_x.at[s, :, high], near_x),
            "sum_y_low": lambda: (p.at[at(4), low], full_y.at[s, :, low], near_y),
            "sum_y_high": lambda: (p.at[at(4), high], full_y.at[s, :, high], near_y),
        }[kind]()

    def copy(kind, s):
        src, dst, target = ends(kind, s)
        return pltpu.make_async_remote_copy(
            src_ref=src,
            dst_ref=dst,
            send_sem=send_sem.at[numbers[kind, s]],
            recv_sem=recv_sem.at[numbers[kind, s]],
            device_id={"expert": target},
            device_id_type=pl.DeviceIdType.MESH,
        )

    moves = {step: copy(*step) for step in numbers}

    residual = tokens[0].astype(jnp.float32)
    normed = (
        residual
        * lax.rsqrt(jnp.mean(residual * residual, -1, keepdims=True) + EPSILON)
        * gain[...].astype(jnp.float32)
    ).astype(jnp.bfloat16)
    rows[0, at(0), :] = normed
    pl.semaphore_wait(barrier, len(partners))

    def own_sum(s, q, columns):
        return part[s, at(q), columns].astype(jnp.float32) + core_in[s, at(q), columns].astype(
            jnp.float32
        )

    def keep(s, q, columns, total):
        part[s, at(q), columns] = total.astype(jnp.bfloat16)

    def plane_sum(s, columns):
        return (
            own_sum(s, 0, columns)
            + full_x[s, :, columns].astype(jnp.float32)
            + full_y[s, :, columns].astype(jnp.float32)
        )

    def compute(s):
        both = jnp.dot(rows[s], w_in[...], preferred_element_type=jnp.float32)
        ff = both.shape[1] // 2
        gate, upward = both[:, :ff], both[:, ff:]
        hidden = (gate / (1.0 + jnp.exp(-gate)) * upward).astype(jnp.bfloat16)
        for kind, begin, end in (("swap_low", 0, half), ("swap_high", half, width)):
            step = 2 * BLOCK
            for first in range(begin, end, step):
                columns = slice(first, min(first + step, end))
                part[s, :, columns] = jnp.dot(
                    hidden, w_down[:, columns], preferred_element_type=jnp.float32
                ).astype(jnp.bfloat16)
            moves[kind, s].start()

    def prepare():
        for load in loads:
            load.wait()
        ff = down_values.shape[1]
        for k in range(width // BLOCK):
            block = slice(k * BLOCK, (k + 1) * BLOCK)
            w_in[block, :ff] = (gate_raw[block, :].astype(jnp.float32) * gate_scale[0, k]).astype(jnp.bfloat16)
            w_in[block, ff:] = (up_raw[block, :].astype(jnp.float32) * up_scale[0, k]).astype(jnp.bfloat16)
            w_down[:, block] = (down_raw[:, block].astype(jnp.float32) * down_scale[0, k]).astype(jnp.bfloat16)

        logits = lax.dot_general(
            router[...], normed, (((1,), (1,)), ((), ())), preferred_element_type=jnp.float32
        )
        affinity = 1.0 / (1.0 + jnp.exp(-logits))
        index = lax.broadcasted_iota(jnp.int32, (experts, tok_dev), 0)
        chosen_map = jnp.zeros((experts, tok_dev), jnp.float32)
        for k in range(picks.shape[0]):
            chosen_map += jnp.where(picks[k : k + 1, :] == index, affinity, 0.0)
        coef = ROUTE_SCALE * chosen_map / jnp.sum(chosen_map, 0, keepdims=True)
        plane = me // group
        diagonal = lax.broadcasted_iota(jnp.int32, (tok_dev, tok_dev), 0) == lax.broadcasted_iota(
            jnp.int32, (tok_dev, tok_dev), 1
        )

        def share(s):
            row = jnp.sum(jnp.where(index == flipped(plane, s), coef, 0.0), 0, keepdims=True)
            return jnp.sum(jnp.where(diagonal, row, 0.0), -1, keepdims=True)

        return [share(s) for s in range(experts)]

    shares = None
    needs, order = plan(experts)
    waited, left = set(), {"finl": experts, "finh": experts}
    for kind, s in order:
        if needs[kind, s] and shares is None:
            shares = prepare()
        for need in needs[kind, s]:
            if need in moves and need not in waited:
                moves[need].wait_recv()
                waited.add(need)
        if kind == "comp":
            compute(s)
            continue
        if kind.startswith("fin"):
            columns = slice(0, half) if kind == "finl" else slice(half, width)
            if s:
                term = shares[s] * homed[s, :, columns].astype(jnp.float32)
            else:
                term = shares[s] * plane_sum(s, columns)
            if left[kind] == experts:
                term += tokens[0, :, columns].astype(jnp.float32)
            else:
                term += acc[:, columns]
            left[kind] -= 1
            if left[kind]:
                acc[:, columns] = term
            else:
                out[0, :, columns] = term.astype(jnp.bfloat16)
            continue
        if kind == "diag_low":
            keep(s, 6, low, own_sum(s, 6, low))
        elif kind == "sum_x_low":
            keep(s, 2, low, own_sum(s, 2, low))
        elif kind == "diag_high":
            keep(s, 6, high, own_sum(s, 6, high))
        elif kind == "sum_y_high":
            keep(s, 4, high, own_sum(s, 4, high))
        elif kind == "sum_y_low":
            keep(s, 4, low, own_sum(s, 4, low) + diag_x[s].astype(jnp.float32))
        elif kind == "sum_x_high":
            keep(s, 2, high, own_sum(s, 2, high) + diag_y[s].astype(jnp.float32))
        elif kind == "homel":
            keep(s, 0, low, plane_sum(s, low))
        elif kind == "homeh":
            keep(s, 0, high, plane_sum(s, high))
        moves[kind, s].start()

    for move in moves.values():
        move.wait_send()


def on_device(
    tokens,
    routes,
    norm_gain,
    router,
    gate_values,
    gate_scale,
    up_values,
    up_scale,
    down_values,
    down_scale,
):
    tok_dev, width = tokens.shape[1:]
    experts = router.shape[2]
    group = lax.axis_size("expert") // experts
    assert group == len(ORDER) and experts & (experts - 1) == 0
    ff = down_values.shape[1]
    half = width // BLOCK // 2 * BLOCK
    smem = pl.BlockSpec(memory_space=pltpu.SMEM)
    anywhere = pl.BlockSpec(memory_space=pl.ANY)
    vmem = pl.BlockSpec(memory_space=pltpu.VMEM)
    copies = len(kinds(experts))

    def buffer(*shape):
        return pltpu.VMEM(shape, jnp.bfloat16)

    result = pl.pallas_call(
        functools.partial(kernel, experts, group),
        out_shape=jax.ShapeDtypeStruct(tokens.shape, jnp.bfloat16),
        in_specs=[smem] * 3 + [vmem] * 4 + [anywhere] * 3,
        out_specs=vmem,
        scratch_shapes=[
            buffer(experts, group * tok_dev, width),
            buffer(experts, group * tok_dev, width),
            buffer(experts, group // 2 * tok_dev, width),
            buffer(experts, tok_dev, half),
            buffer(experts, tok_dev, width - half),
            buffer(experts, tok_dev, width),
            buffer(experts, tok_dev, width),
            buffer(experts, tok_dev, width),
            buffer(width, 2 * ff),
            buffer(ff, width),
            buffer(width, ff),
            buffer(width, ff),
            buffer(ff, width),
            pltpu.VMEM((tok_dev, width), jnp.float32),
            pltpu.SemaphoreType.DMA((copies,)),
            pltpu.SemaphoreType.DMA((copies,)),
            pltpu.SemaphoreType.DMA((3,)),
        ],
        compiler_params=pltpu.CompilerParams(
            collective_id=0, has_side_effects=True, vmem_limit_bytes=60 << 20
        ),
        name="moe_layer",
    )(
        jnp.swapaxes(gate_scale[0], 0, 1),
        jnp.swapaxes(up_scale[0], 0, 1),
        down_scale[0],
        tokens,
        jnp.swapaxes(routes[0], 0, 1),
        norm_gain,
        jnp.swapaxes(router[0], 0, 1),
        gate_values,
        up_values,
        down_values,
    )
    segments = lax.axis_size("segment")
    if segments > 1:
        result = lax.ppermute(
            result, "segment", [(s, (s + 1) % segments) for s in range(segments)]
        )
    return result


def solution(mesh):
    return jax.shard_map(
        on_device,
        mesh=mesh,
        in_specs=(
            P("segment", "expert", None),
            P("segment", "expert", None),
            P("segment", None),
            P("segment", None, None),
            P("segment", None, "expert"),
            P("segment", None, "expert"),
            P("segment", None, "expert"),
            P("segment", None, "expert"),
            P("segment", "expert", None),
            P("segment", "expert", None),
        ),
        out_specs=P("segment", "expert", None),
        check_vma=False,
    )
```
